768 devices in a mesh: ka: 48 (over z, x_lo, core), ba: 16 (over y, x_hi).
Axes of the slice: x: 4 (x_hi: 2, x_lo: 2; x = x_hi * 2 + x_lo), y: 8, z: 12, core: 2. Of those that a mesh axis runs over, the one named last changes fastest.
Arguments:
- orbitals: bfloat16 [48, 16, 2, 32768], P('ka', 'ba'), may hold values from -6 to 6
- kpoint_coords: int32 [48, 3], replicated, may hold values from 0 to 3
Outputs:
- exchange_field: float32 [48, 16, 2, 32768], P('ka', 'ba')
The draws below stay inside these ranges and needn't reach their ends.
All inputs are finite; a program needn't handle non-finite values.
Results may differ from the reference program's by a relative error of at most 0.0074.
Values may be sent and summed in bfloat16 or wider, within the bound.
A program may use at most 32 MiB of HBM per device.

```python
import math
import jax
import jax.numpy as jnp
from jax import lax

GRID = 32
CELLS = 32768
BANDS_DEV = 1
BANDS = 16
KPTS = 48
SHIFT = 12
MATCHES = 3
N_BA = 16


def with_ends(drawn, own_key, least, largest):
    spot = [jax.random.randint(jax.random.fold_in(own_key, axis), (), 0, length) for axis, length in enumerate(drawn.shape)]
    widest = drawn.shape.index(max(drawn.shape))
    neighbour = spot[:widest] + [(spot[widest] + 1) % drawn.shape[widest]] + spot[widest + 1:]
    return drawn.at[tuple(spot)].set(least).at[tuple(neighbour)].set(largest)


def level_of(rng, dims, pieces, least, largest):
    level, own = 1.0, jax.random.fold_in(rng, 6)
    for position, blocks in pieces:
        heights = jnp.exp(jax.random.uniform(jax.random.fold_in(own, position), (blocks,), jnp.float32, least / len(pieces), largest / len(pieces)))
        level = level * jnp.repeat(heights, dims[position] // blocks).reshape([-1 if axis == position else 1 for axis in range(len(dims))])
    return level


def bell_draw(own_key, dims, width, bound, split=(), kind=jnp.bfloat16):
    array = width * jax.random.normal(own_key, dims, jnp.float32)
    if split:
        array = array * level_of(own_key, dims, split, -0.22, 0.18)
    return jnp.clip(array, -bound, bound).astype(kind)


def setup_inputs(seed: int = 0) -> dict:
    keys = jax.random.split(jax.random.key(seed), 3)
    return {
        "orbitals": bell_draw(keys[0], (KPTS, BANDS, 2, CELLS), 1.0, 6.0, ((0, 48), (1, 16))),
        "kpoint_coords": with_ends(jax.random.randint(keys[1], (KPTS, 3), 0, 4), jax.random.fold_in(keys[1], 1), 0, 3).astype(jnp.int32),
    }


def wave_tables(grid, sign):
    index = jnp.arange(grid, dtype=jnp.int32)
    phase = (index[:, None] * index[None, :]) % grid
    angle = phase.astype(jnp.float32) * (2.0 * math.pi / grid)
    cosine = jnp.cos(angle)
    sine = sign * jnp.sin(angle)
    table = jnp.stack([jnp.stack([cosine, sine]), jnp.stack([-sine, cosine])])
    return table.astype(jnp.bfloat16)


def one_pass(field, table, grid):
    count = field.shape[0]
    shaped = field.reshape(count, 2, grid * grid, grid).astype(jnp.float32)
    result = jnp.einsum("pcme,dcfe->pdfm", shaped, table.astype(jnp.float32))
    return result.reshape(count, 2, grid ** 3)


def transform(field, table, grid):
    first = one_pass(field, table, grid).astype(jnp.bfloat16)
    second = one_pass(first, table, grid).astype(jnp.bfloat16)
    return one_pass(second, table, grid)


def coulomb_kernel(offset, grid):
    index = jnp.arange(grid, dtype=jnp.int32)
    signed = jnp.where(index < grid // 2, index, index - grid).astype(jnp.float32)
    along_x = signed[:, None, None] + offset[0]
    along_y = signed[None, :, None] + offset[1]
    along_z = signed[None, None, :] + offset[2]
    square = along_x * along_x + along_y * along_y + along_z * along_z
    return ((32.0 / (grid ** 3)) / (square + 0.25)).reshape(grid ** 3)


def pair_density(former, latter):
    f_real = former[..., :, None, 0, :].astype(jnp.float32)
    f_imag = former[..., :, None, 1, :].astype(jnp.float32)
    l_real = latter[..., None, :, 0, :].astype(jnp.float32)
    l_imag = latter[..., None, :, 1, :].astype(jnp.float32)
    real = l_real * f_real + l_imag * f_imag
    imag = l_real * f_imag - l_imag * f_real
    return jnp.stack([real, imag], axis=-2).astype(jnp.bfloat16)


def coulomb_fields(former, latter, kernel, forward, inverse, grid):
    density = pair_density(former, latter)
    flat = density.reshape(-1, 2, grid ** 3)
    spectrum = transform(flat, forward, grid)
    screened = (spectrum * kernel).astype(jnp.bfloat16)
    return transform(screened, inverse, grid).reshape(density.shape)


def apply_fields(fields, latter):
    w_real = fields[..., 0, :]
    w_imag = fields[..., 1, :]
    l_real = latter[..., None, :, 0, :].astype(jnp.float32)
    l_imag = latter[..., None, :, 1, :].astype(jnp.float32)
    real = -jnp.sum(l_real * w_real - l_imag * w_imag, axis=-2)
    imag = -jnp.sum(l_real * w_imag + l_imag * w_real, axis=-2)
    return jnp.stack([real, imag], axis=-2)


def back_fields(fields, former):
    w_real = fields[..., 0, :]
    w_imag = fields[..., 1, :]
    f_real = former[..., :, None, 0, :].astype(jnp.float32)
    f_imag = former[..., :, None, 1, :].astype(jnp.float32)
    real = -jnp.sum(f_real * w_real + f_imag * w_imag, axis=-3)
    imag = -jnp.sum(f_imag * w_real - f_real * w_imag, axis=-3)
    return jnp.stack([real, imag], axis=-2)


def reference(orbitals, kpoint_coords):
    groups = N_BA
    cells = CELLS
    forward = wave_tables(GRID, 1.0)
    inverse = wave_tables(GRID, -1.0)
    coords = kpoint_coords.astype(jnp.float32)
    shaped = orbitals.reshape(KPTS, groups, BANDS_DEV, 2, cells)
    group_ids = jnp.arange(groups, dtype=jnp.int32)

    def visit(number, result):
        here = jnp.asarray(number).astype(jnp.int32)
        source = ((here - SHIFT) % KPTS).astype(jnp.int32)
        own = lax.dynamic_index_in_dim(shaped, here, 0, keepdims=False)
        far = lax.dynamic_index_in_dim(shaped, source, 0, keepdims=False)
        offset = (lax.dynamic_index_in_dim(coords, here, 0, keepdims=False)
                  - lax.dynamic_index_in_dim(coords, source, 0, keepdims=False)) / 4.0
        kernel = coulomb_kernel(offset, GRID)
        gain = jnp.zeros((groups, BANDS_DEV, 2, cells), jnp.float32)
        back = jnp.zeros((groups, BANDS_DEV, 2, cells), jnp.float32)
        for matching in range(MATCHES):
            partner_ids = jnp.bitwise_xor(group_ids, jnp.int32(1 << matching))
            partner = far[partner_ids]
            fields = coulomb_fields(own, partner, kernel, forward, inverse, GRID)
            gain = gain + apply_fields(fields, partner)
            rounded = lax.optimization_barrier(back_fields(fields, own).astype(jnp.bfloat16))
            back = back + rounded.astype(jnp.float32)[partner_ids]
        row_here = lax.dynamic_index_in_dim(result, here, 0, keepdims=False)
        result = lax.dynamic_update_index_in_dim(result, row_here + gain, here, 0)
        row_source = lax.dynamic_index_in_dim(result, source, 0, keepdims=False)
        return lax.dynamic_update_index_in_dim(result, row_source + back, source, 0)

    start = jnp.zeros((KPTS, groups, BANDS_DEV, 2, cells), jnp.float32)
    final = lax.fori_loop(0, KPTS, visit, start)
    return final.reshape(KPTS, BANDS, 2, cells)
```

```python
import functools
import math

import jax
import jax.numpy as jnp
import numpy as np
from jax import lax
from jax.experimental import pallas as pl
from jax.experimental.pallas import tpu as pltpu
from jax.sharding import PartitionSpec as P

GRID = 32
ROWS = 256
LANES = 128
CHUNKS = 8
PART = ROWS // CHUNKS
MATCHES = 3
MESH = pl.DeviceIdType.MESH
F32 = jnp.float32
BF16 = jnp.bfloat16


def waves():
    row = np.arange(ROWS)
    lane = np.arange(LANES)
    row_phase = (np.outer(row // 8, row // 8) + 4 * np.outer(row % 8, row % 8)) % GRID
    lane_phase = (8 * np.outer(lane // GRID, lane // GRID) + np.outer(lane % GRID, lane % GRID)) % GRID
    tables = []
    for sign in (1.0, -1.0):
        cosine, sine = (f(row_phase * (2.0 * math.pi / GRID)) for f in (np.cos, np.sin))
        sine = sign * sine
        tables.append(np.block([[cosine, sine], [-sine, cosine]]))
        cosine, sine = (f(lane_phase * (2.0 * math.pi / GRID)) for f in (np.cos, np.sin))
        sine = sign * sine
        tables.append(np.block([[cosine, -sine], [sine, cosine]]))
    return [jnp.asarray(table.astype(np.float32)).astype(BF16) for table in tables]


def part(chunk):
    return pl.ds(chunk * PART, PART)


def signed(index):
    return jnp.where(index < GRID // 2, index, index - GRID).astype(F32)


def coulomb(q, flipped):
    row = lax.broadcasted_iota(jnp.int32, (ROWS, LANES), 0)
    lane = lax.broadcasted_iota(jnp.int32, (ROWS, LANES), 1)
    indices = (row // 8, row % 8 + 8 * (lane // GRID), lane % GRID)
    square = jnp.zeros((ROWS, LANES), F32)
    for index, offset in zip(indices, q):
        if flipped:
            index = (GRID - index) % GRID
        along = signed(index) + offset
        square = square + along * along
    return (32.0 / GRID**3) / (square + 0.25)


def kernel(kpoints, u_ref, coords_ref, rows_f, lanes_f, rows_i, lanes_i, out_ref,
           tab_rf, tab_lf, tab_ri, tab_li, far, near, field, kern, xs, zs, ys,
           tab_sem, far_send, far_recv, near_send, near_recv):
    steps = kpoints // 4
    ka = lax.axis_index("ka")
    ba = lax.axis_index("ba")
    above = lax.rem(ka + steps, kpoints)
    below = lax.rem(ka + kpoints - steps, kpoints)
    bit0 = lax.rem(ba, 2)
    bit1 = lax.rem(ba // 2, 2)
    bit2 = lax.rem(ba // 4, 2)
    partners = (ba + 1 - 2 * bit0, ba + 2 - 4 * bit1, ba + 4 - 8 * bit2)

    loads = []
    for n, (source, target) in enumerate(((rows_f, tab_rf), (lanes_f, tab_lf), (lanes_i, tab_li), (rows_i, tab_ri))):
        loads.append(pltpu.make_async_copy(source, target, tab_sem.at[n]))
        loads[-1].start()

    barrier = pltpu.get_barrier_semaphore()
    for k in (above, below):
        pl.semaphore_signal(barrier, inc=1, device_id=(k, ba), device_id_type=MESH)
    for b in partners:
        pl.semaphore_signal(barrier, inc=1, device_id=(ka, b), device_id_type=MESH)
    pl.semaphore_wait(barrier, 2 + MATCHES)

    def far_copy(way, chunk):
        return pltpu.make_async_remote_copy(
            src_ref=u_ref.at[:, part(chunk)], dst_ref=far.at[way, :, part(chunk)],
            send_sem=far_send.at[way, chunk], recv_sem=far_recv.at[way, chunk],
            device_id=((above, below)[way], ba), device_id_type=MESH)

    def near_copy(way, match, chunk):
        return pltpu.make_async_remote_copy(
            src_ref=far.at[way, :, part(chunk)], dst_ref=near.at[way, match, :, part(chunk)],
            send_sem=near_send.at[way, match, chunk], recv_sem=near_recv.at[way, match, chunk],
            device_id=(ka, partners[match]), device_id_type=MESH)

    for chunk in range(CHUNKS):
        for way in range(2):
            far_copy(way, chunk).start()

    def coord(k, axis):
        return coords_ref[axis, k].astype(F32)

    kern[0] = coulomb([(coord(ka, a) - coord(below, a)) * 0.25 for a in range(3)], False)
    kern[1] = coulomb([(coord(above, a) - coord(ka, a)) * 0.25 for a in range(3)], True)
    f1 = lax.broadcasted_iota(jnp.int32, (PART, LANES), 0) % 8
    y_lo = lax.broadcasted_iota(jnp.int32, (PART, LANES), 1) // GRID
    angle = (f1 * y_lo).astype(F32) * (2.0 * math.pi / GRID)
    tw_cos, tw_sin = jnp.cos(angle), jnp.sin(angle)

    for chunk in range(CHUNKS):
        for way in range(2):
            far_copy(way, chunk).wait_recv()
            for match in range(MATCHES):
                near_copy(way, match, chunk).start()

    for load in loads:
        load.wait()

    def edge(way, match, first):
        v = near.at[way, match]
        for c in range(CHUNKS):
            ur, ui = u_ref[0, part(c)].astype(F32), u_ref[1, part(c)].astype(F32)
            vr, vi = v[0, part(c)].astype(F32), v[1, part(c)].astype(F32)
            xs[part(c), :] = (ur * vr + ui * vi).astype(BF16)
            xs[pl.ds(ROWS + c * PART, PART), :] = (ui * vr - ur * vi).astype(BF16)
        zs[...] = jnp.dot(tab_rf[...], xs[...], preferred_element_type=F32)
        for c in range(CHUNKS):
            zr, zi = zs[part(c), :], zs[pl.ds(ROWS + c * PART, PART), :]
            ys[part(c), :LANES] = (zr * tw_cos + zi * tw_sin).astype(BF16)
            ys[part(c), LANES:] = (zi * tw_cos - zr * tw_sin).astype(BF16)
        field[...] = jnp.dot(ys[...], tab_lf[...], preferred_element_type=F32)
        for c in range(CHUNKS):
            scale = kern[way, part(c), :]
            ys[part(c), :LANES] = (field[part(c), :LANES] * scale).astype(BF16)
            ys[part(c), LANES:] = (field[part(c), LANES:] * scale).astype(BF16)
        field[...] = jnp.dot(ys[...], tab_li[...], preferred_element_type=F32)
        for c in range(CHUNKS):
            fr, fi = field[part(c), :LANES], field[part(c), LANES:]
            xs[part(c), :] = (fr * tw_cos - fi * tw_sin).astype(BF16)
            xs[pl.ds(ROWS + c * PART, PART), :] = (fi * tw_cos + fr * tw_sin).astype(BF16)
        zs[...] = jnp.dot(tab_ri[...], xs[...], preferred_element_type=F32)
        for c in range(CHUNKS):
            vr, vi = v[0, part(c)].astype(F32), v[1, part(c)].astype(F32)
            wr, wi = zs[part(c), :], zs[pl.ds(ROWS + c * PART, PART), :]
            real, imag = vi * wi - vr * wr, -(vr * wi + vi * wr)
            if not first:
                real = out_ref[0, part(c), :] + real
                imag = out_ref[1, part(c), :] + imag
            out_ref[0, part(c), :] = real
            out_ref[1, part(c), :] = imag

    first = True
    for way in range(2):
        for match in range(MATCHES):
            for chunk in range(CHUNKS):
                near_copy(way, match, chunk).wait_recv()
            edge(way, match, first)
            first = False

    for chunk in range(CHUNKS):
        for way in range(2):
            far_copy(way, chunk).wait_send()
            for match in range(MATCHES):
                near_copy(way, match, chunk).wait_send()


def per_device(orbitals, kpoint_coords):
    kpoints = lax.axis_size("ka")
    own = orbitals.reshape(2, ROWS, LANES)
    rows_f, lanes_f, rows_i, lanes_i = waves()
    vmem = pl.BlockSpec(memory_space=pltpu.VMEM)
    whole = pl.BlockSpec(memory_space=pl.ANY)
    sems = pltpu.SemaphoreType.DMA
    out = pl.pallas_call(
        functools.partial(kernel, kpoints),
        out_shape=jax.ShapeDtypeStruct((2, ROWS, LANES), F32),
        in_specs=[vmem, pl.BlockSpec(memory_space=pltpu.SMEM), whole, whole, whole, whole],
        out_specs=vmem,
        scratch_shapes=[
            pltpu.VMEM((2 * ROWS, 2 * ROWS), BF16),
            pltpu.VMEM((2 * LANES, 2 * LANES), BF16),
            pltpu.VMEM((2 * ROWS, 2 * ROWS), BF16),
            pltpu.VMEM((2 * LANES, 2 * LANES), BF16),
            pltpu.VMEM((2, 2, ROWS, LANES), BF16),
            pltpu.VMEM((2, MATCHES, 2, ROWS, LANES), BF16),
            pltpu.VMEM((ROWS, 2 * LANES), F32),
            pltpu.VMEM((2, ROWS, LANES), F32),
            pltpu.VMEM((2 * ROWS, LANES), BF16),
            pltpu.VMEM((2 * ROWS, LANES), F32),
            pltpu.VMEM((ROWS, 2 * LANES), BF16),
            sems((4,)),
            sems((2, CHUNKS)),
            sems((2, CHUNKS)),
            sems((2, MATCHES, CHUNKS)),
            sems((2, MATCHES, CHUNKS)),
        ],
        compiler_params=pltpu.CompilerParams(collective_id=0, has_side_effects=True),
    )(own, kpoint_coords.T, rows_f, lanes_f, rows_i, lanes_i)
    return out.reshape(1, 1, 2, GRID**3)


def solution(mesh):
    return jax.shard_map(
        per_device,
        mesh=mesh,
        in_specs=(P("ka", "ba", None, None), P()),
        out_specs=P("ka", "ba", None, None),
        check_vma=False,
    )
```

```python
import functools
import math

import jax
import jax.numpy as jnp
import numpy as np
from jax import lax
from jax.experimental import pallas as pl
from jax.experimental.pallas import tpu as pltpu
from jax.sharding import PartitionSpec as P

GRID = 32
ROWS = 256
LANES = 128
CHUNKS = 8
COLLECTIVE = 0
VMEM = 24 * 2**20
PART = ROWS // CHUNKS
HOLD = 4
MATCHES = 3
MESH = pl.DeviceIdType.MESH
F32 = jnp.float32
BF16 = jnp.bfloat16


def waves():
    row = np.arange(ROWS)
    lane = np.arange(LANES)
    row_phase = (np.outer(row // 8, row // 8) + 4 * np.outer(row % 8, row % 8)) % GRID
    lane_phase = (8 * np.outer(lane // GRID, lane // GRID) + np.outer(lane % GRID, lane % GRID)) % GRID
    tables = []
    for sign in (1.0, -1.0):
        cosine, sine = (f(row_phase * (2.0 * math.pi / GRID)) for f in (np.cos, np.sin))
        sine = sign * sine
        tables.append(np.block([[cosine, sine], [-sine, cosine]]))
        cosine, sine = (f(lane_phase * (2.0 * math.pi / GRID)) for f in (np.cos, np.sin))
        sine = sign * sine
        tables.append(np.block([[cosine, -sine], [sine, cosine]]))
    angle = np.outer(np.arange(PART) % 8, lane // GRID) * (2.0 * math.pi / GRID)
    turn = jnp.asarray(np.stack([np.cos(angle), np.sin(angle)]).astype(np.float32))
    return [jnp.asarray(table.astype(np.float32)).astype(BF16) for table in tables] + [turn]


def part(chunk):
    return pl.ds(chunk * PART, PART)


def pairs(chunk):
    return pl.ds(chunk * 2 * PART, 2 * PART)


def reals(chunk):
    return pl.ds(chunk * 2 * PART, PART, stride=2)


def imags(chunk):
    return pl.ds(chunk * 2 * PART + 1, PART, stride=2)


def signed(index):
    return jnp.where(index < GRID // 2, index, index - GRID).astype(F32)


def coulomb(q, flipped):
    row = lax.broadcasted_iota(jnp.int32, (ROWS, LANES), 0)
    lane = lax.broadcasted_iota(jnp.int32, (ROWS, LANES), 1)
    indices = (row // 8, row % 8 + 8 * (lane // GRID), lane % GRID)
    square = jnp.zeros((ROWS, LANES), F32)
    for index, offset in zip(indices, q):
        if flipped:
            index = (GRID - index) % GRID
        along = signed(index) + offset
        square = square + along * along
    return (32.0 / GRID**3) / (square + 0.25)


def kernel(kpoints, u_hbm, coords_hbm, rows_f, lanes_f, rows_i, lanes_i, turn, out_ref,
           tab_rf, tab_lf, tab_li, tab_ri, tab_turn, coords, u_raw, far, near, own, raw, total, kern, xs, zs, ys, fs,
           tab_sem, far_send, far_recv, near_send, near_recv, ready):
    steps = kpoints // 4
    ka = lax.axis_index("ka")
    ba = lax.axis_index("ba")
    quarter = ka // steps
    first = lax.rem(quarter + 3, 4) // 2
    last = 1 - first
    bit0 = lax.rem(ba, 2)
    bit1 = lax.rem(ba // 2, 2)
    bit2 = lax.rem(ba // 4, 2)
    partners = (ba + 1 - 2 * bit0, ba + 2 - 4 * bit1, ba + 4 - 8 * bit2)

    def beside(side):
        return lax.rem(ka + kpoints + (2 * side - 1) * steps, kpoints)

    loads = []
    for n, (source, target) in enumerate(((u_hbm, u_raw), (coords_hbm, coords), (turn, tab_turn), (rows_f, tab_rf),
                                          (lanes_f, tab_lf), (lanes_i, tab_li), (rows_i, tab_ri))):
        loads.append(pltpu.make_async_copy(source, target, tab_sem.at[n]))

    def signal(semaphore, k, b):
        pl.semaphore_signal(semaphore, inc=1, device_id=(k, b), device_id_type=MESH)

    barrier = pltpu.get_barrier_semaphore()

    @pl.when(quarter == 0)
    def _():
        signal(barrier, beside(first), ba)

    @pl.when(quarter != 3)
    def _():
        signal(barrier, beside(last), ba)

    for b in partners:
        signal(barrier, ka, b)
    for load in loads:
        load.start()
    pl.semaphore_wait(barrier, MATCHES + (quarter + 2) // 3 + quarter // 3)

    @pl.when(quarter != 0)
    def _():
        signal(ready.at[quarter // 2], beside(first), ba)

    @pl.when(quarter == 3)
    def _():
        signal(ready.at[1], beside(last), ba)

    def far_copy(side, chunk):
        return pltpu.make_async_remote_copy(
            src_ref=u_hbm.at[pairs(chunk)], dst_ref=far.at[1 - side, pairs(chunk)],
            send_sem=far_send.at[side, chunk], recv_sem=far_recv.at[1 - side, chunk],
            device_id=(beside(side), ba), device_id_type=MESH)

    def far_arrived(side, chunk):
        pltpu.make_async_remote_copy(
            src_ref=u_hbm.at[pairs(chunk)], dst_ref=far.at[side, pairs(chunk)],
            send_sem=far_send.at[side, chunk], recv_sem=far_recv.at[side, chunk],
            device_id=(beside(side), ba), device_id_type=MESH).wait_recv()

    def near_copy(side, match, chunk):
        return pltpu.make_async_remote_copy(
            src_ref=far.at[side, pairs(chunk)], dst_ref=near.at[side, match, pairs(chunk)],
            send_sem=near_send.at[side, match, chunk], recv_sem=near_recv.at[side, match, chunk],
            device_id=(ka, partners[match]), device_id_type=MESH)

    def send(side):
        for chunk in range(CHUNKS):
            far_copy(side, chunk).start()

    def forward(side, chunk):
        far_arrived(side, chunk)
        for match in reversed(range(MATCHES)):
            near_copy(side, match, chunk).start()

    @pl.when(quarter == 0)
    def _():
        pl.semaphore_wait(ready.at[0], 1)

    send(first)

    @pl.when(quarter == 2)
    def _():
        pl.semaphore_wait(ready.at[1], 1)

    @pl.when(quarter >= 2)
    def _():
        send(last)

    loads[1].wait()

    def coord(k, axis):
        return coords[axis, k].astype(F32)

    below, above = beside(0), beside(1)
    kern[0] = coulomb([(coord(ka, a) - coord(below, a)) * 0.25 for a in range(3)], False)
    kern[1] = coulomb([(coord(above, a) - coord(ka, a)) * 0.25 for a in range(3)], True)
    loads[0].wait()
    for c in range(CHUNKS):
        raw[0, pairs(c), :] = u_raw[pairs(c), :].astype(F32)
    for c in range(CHUNKS):
        own[0, part(c), :] = raw[0, reals(c), :]
        own[1, part(c), :] = raw[0, imags(c), :]
    for load in loads[2:]:
        load.wait()

    for chunk in range(HOLD):
        forward(first, chunk)

    @pl.when(quarter < 2)
    def _():
        pl.semaphore_wait(ready.at[1], 1)
        send(last)

    for chunk in range(HOLD, CHUNKS):
        forward(first, chunk)

    def lanes(match):
        return pl.ds(match * LANES, LANES)

    def rows(match, c):
        return pl.ds(match * ROWS + c * PART, PART)

    def densities(side):
        for match in range(MATCHES):
            for chunk in range(CHUNKS):
                near_copy(side, match, chunk).wait_recv()
            for c in range(CHUNKS):
                raw[match, pairs(c), :] = near[side, match, pairs(c), :].astype(F32)
            for c in range(CHUNKS):
                ur, ui = own[0, part(c), :], own[1, part(c), :]
                vr, vi = raw[match, reals(c), :], raw[match, imags(c), :]
                xs[part(c), lanes(match)] = (ur * vr + ui * vi).astype(BF16)
                xs[part(CHUNKS + c), lanes(match)] = (ui * vr - ur * vi).astype(BF16)

    def turn_in():
        for match in range(MATCHES):
            for c in range(CHUNKS):
                zr, zi = zs[part(c), lanes(match)], zs[part(CHUNKS + c), lanes(match)]
                ys[rows(match, c), :LANES] = (zr * tab_turn[0] + zi * tab_turn[1]).astype(BF16)
                ys[rows(match, c), LANES:] = (zi * tab_turn[0] - zr * tab_turn[1]).astype(BF16)

    def screen(side):
        for match in range(MATCHES):
            for c in range(CHUNKS):
                scale = kern[side, part(c), :]
                ys[rows(match, c), :LANES] = (fs[rows(match, c), :LANES] * scale).astype(BF16)
                ys[rows(match, c), LANES:] = (fs[rows(match, c), LANES:] * scale).astype(BF16)

    def turn_back():
        for match in range(MATCHES):
            for c in range(CHUNKS):
                fr, fi = fs[rows(match, c), :LANES], fs[rows(match, c), LANES:]
                xs[part(c), lanes(match)] = (fr * tab_turn[0] - fi * tab_turn[1]).astype(BF16)
                xs[part(CHUNKS + c), lanes(match)] = (fi * tab_turn[0] + fr * tab_turn[1]).astype(BF16)

    def product(target, left, right):
        target[...] = jnp.dot(left[...], right[...], preferred_element_type=F32)

    def apply(final):
        for c in range(CHUNKS):
            real = total[0, part(c), :] if final else jnp.zeros((PART, LANES), F32)
            imag = total[1, part(c), :] if final else jnp.zeros((PART, LANES), F32)
            for match in range(MATCHES):
                vr, vi = raw[match, reals(c), :], raw[match, imags(c), :]
                wr, wi = zs[part(c), lanes(match)], zs[part(CHUNKS + c), lanes(match)]
                real = real + (vi * wi - vr * wr)
                imag = imag - (vr * wi + vi * wr)
            if final:
                out_ref[reals(c), :] = real
                out_ref[imags(c), :] = imag
            else:
                total[0, part(c), :] = real
                total[1, part(c), :] = imag

    def stages(side, final):
        return (
            lambda: densities(side),
            lambda: product(zs, tab_rf, xs),
            turn_in,
            lambda: product(fs, ys, tab_lf),
            lambda: screen(side),
            lambda: product(fs, ys, tab_li),
            lambda: (turn_back(), product(zs, tab_ri, xs)),
            lambda: apply(final),
        )

    for chunk, stage in enumerate(stages(first, False)):
        forward(last, chunk)
        stage()
    for stage in stages(last, True):
        stage()

    for side in range(2):
        for chunk in range(CHUNKS):
            far_copy(side, chunk).wait_send()
            for match in range(MATCHES):
                near_copy(side, match, chunk).wait_send()


def per_device(orbitals, kpoint_coords):
    kpoints = lax.axis_size("ka")
    own = orbitals.reshape(2, ROWS, LANES).transpose(1, 0, 2).reshape(2 * ROWS, LANES)
    whole = pl.BlockSpec(memory_space=pltpu.HBM)
    sems = pltpu.SemaphoreType.DMA
    tables = waves()
    out = pl.pallas_call(
        functools.partial(kernel, kpoints),
        out_shape=jax.ShapeDtypeStruct((2 * ROWS, LANES), F32),
        in_specs=[whole] * (2 + len(tables)),
        out_specs=pl.BlockSpec(memory_space=pltpu.VMEM),
        scratch_shapes=[
            pltpu.VMEM((2 * ROWS, 2 * ROWS), BF16),
            pltpu.VMEM((2 * LANES, 2 * LANES), BF16),
            pltpu.VMEM((2 * LANES, 2 * LANES), BF16),
            pltpu.VMEM((2 * ROWS, 2 * ROWS), BF16),
            pltpu.VMEM((2, PART, LANES), F32),
            pltpu.SMEM((3, kpoints), jnp.int32),
            pltpu.VMEM((2 * ROWS, LANES), BF16),
            pltpu.VMEM((2, 2 * ROWS, LANES), BF16),
            pltpu.VMEM((2, MATCHES, 2 * ROWS, LANES), BF16),
            pltpu.VMEM((2, ROWS, LANES), F32),
            pltpu.VMEM((MATCHES, 2 * ROWS, LANES), F32),
            pltpu.VMEM((2, ROWS, LANES), F32),
            pltpu.VMEM((2, ROWS, LANES), F32),
            pltpu.VMEM((2 * ROWS, MATCHES * LANES), BF16),
            pltpu.VMEM((2 * ROWS, MATCHES * LANES), F32),
            pltpu.VMEM((MATCHES * ROWS, 2 * LANES), BF16),
            pltpu.VMEM((MATCHES * ROWS, 2 * LANES), F32),
            sems((7,)),
            sems((2, CHUNKS)),
            sems((2, CHUNKS)),
            sems((2, MATCHES, CHUNKS)),
            sems((2, MATCHES, CHUNKS)),
            pltpu.SemaphoreType.REGULAR((2,)),
        ],
        compiler_params=pltpu.CompilerParams(collective_id=COLLECTIVE, has_side_effects=True, vmem_limit_bytes=VMEM),
    )(*(pltpu.with_memory_space_constraint(a, pltpu.HBM) for a in (own, kpoint_coords.T, *tables)))
    return out.reshape(ROWS, 2, LANES).transpose(1, 0, 2).reshape(1, 1, 2, GRID**3)


def solution(mesh):
    return jax.shard_map(
        per_device,
        mesh=mesh,
        in_specs=(P("ka", "ba", None, None), P()),
        out_specs=P("ka", "ba", None, None),
        check_vma=False,
    )
```

```python
import functools
import math

import jax
import jax.numpy as jnp
import numpy as np
from jax import lax
from jax.experimental import pallas as pl
from jax.experimental.pallas import tpu as pltpu
from jax.sharding import PartitionSpec as P

GRID = 32
ROWS = 256
LANES = 128
CHUNKS = 8
COLLECTIVE = 0
VMEM = 24 * 2**20
LEADS = (8, 3, 3, 3)
HOLDS = (4, 0, 0)
BLOCKS = 8
PART = ROWS // BLOCKS
MATCHES = 3
MESH = pl.DeviceIdType.MESH
F32 = jnp.float32
BF16 = jnp.bfloat16


def waves():
    row = np.arange(ROWS)
    lane = np.arange(LANES)
    row_phase = (np.outer(row // 8, row // 8) + 4 * np.outer(row % 8, row % 8)) % GRID
    lane_phase = (8 * np.outer(lane // GRID, lane // GRID) + np.outer(lane % GRID, lane % GRID)) % GRID
    tables = []
    for sign in (1.0, -1.0):
        cosine, sine = (f(row_phase * (2.0 * math.pi / GRID)) for f in (np.cos, np.sin))
        sine = sign * sine
        tables.append(np.block([[cosine, sine], [-sine, cosine]]))
        cosine, sine = (f(lane_phase * (2.0 * math.pi / GRID)) for f in (np.cos, np.sin))
        sine = sign * sine
        tables.append(np.block([[cosine, -sine], [sine, cosine]]))
    angle = np.outer(np.arange(PART) % 8, lane // GRID) * (2.0 * math.pi / GRID)
    turn = jnp.asarray(np.stack([np.cos(angle), np.sin(angle)]).astype(np.float32))
    return [jnp.asarray(table.astype(np.float32)).astype(BF16) for table in tables] + [turn]


def part(chunk):
    return pl.ds(chunk * PART, PART)


def piece(chunk):
    return pl.ds(chunk * (2 * ROWS // CHUNKS), 2 * ROWS // CHUNKS)


def pairs(chunk):
    return pl.ds(chunk * 2 * PART, 2 * PART)


def reals(chunk):
    return pl.ds(chunk * 2 * PART, PART, stride=2)


def imags(chunk):
    return pl.ds(chunk * 2 * PART + 1, PART, stride=2)


def signed(index):
    return jnp.where(index < GRID // 2, index, index - GRID).astype(F32)


def coulomb(q, flipped):
    row = lax.broadcasted_iota(jnp.int32, (ROWS, LANES), 0)
    lane = lax.broadcasted_iota(jnp.int32, (ROWS, LANES), 1)
    indices = (row // 8, row % 8 + 8 * (lane // GRID), lane % GRID)
    square = jnp.zeros((ROWS, LANES), F32)
    for index, offset in zip(indices, q):
        if flipped:
            index = (GRID - index) % GRID
        along = signed(index) + offset
        square = square + along * along
    return (32.0 / GRID**3) / (square + 0.25)


def kernel(kpoints, u_hbm, coords_hbm, rows_f, lanes_f, rows_i, lanes_i, turn, out_ref,
           tab_rf, tab_lf, tab_li, tab_ri, tab_turn, coords, u_raw, far, near, own, raw, total, kern, xs, zs, ys, fs,
           tab_sem, far_send, far_recv, near_send, near_recv, ready):
    steps = kpoints // 4
    ka = lax.axis_index("ka")
    ba = lax.axis_index("ba")
    quarter = ka // steps
    first = lax.rem(quarter + 3, 4) // 2
    last = 1 - first
    bit0 = lax.rem(ba, 2)
    bit1 = lax.rem(ba // 2, 2)
    bit2 = lax.rem(ba // 4, 2)
    partners = (ba + 1 - 2 * bit0, ba + 2 - 4 * bit1, ba + 4 - 8 * bit2)

    def beside(side):
        return lax.rem(ka + kpoints + (2 * side - 1) * steps, kpoints)

    loads = []
    for n, (source, target) in enumerate(((u_hbm, u_raw), (coords_hbm, coords), (turn, tab_turn), (rows_f, tab_rf),
                                          (lanes_f, tab_lf), (lanes_i, tab_li), (rows_i, tab_ri))):
        loads.append(pltpu.make_async_copy(source, target, tab_sem.at[n]))

    def signal(semaphore, k, b):
        pl.semaphore_signal(semaphore, inc=1, device_id=(k, b), device_id_type=MESH)

    barrier = pltpu.get_barrier_semaphore()

    @pl.when(quarter == 0)
    def _():
        signal(barrier, beside(first), ba)

    @pl.when(quarter != 3)
    def _():
        signal(barrier, beside(last), ba)

    for b in partners:
        signal(barrier, ka, b)
    for load in loads:
        load.start()
    pl.semaphore_wait(barrier, MATCHES + (quarter + 2) // 3 + quarter // 3)

    @pl.when(quarter != 0)
    def _():
        signal(ready.at[quarter // 2], beside(first), ba)

    @pl.when(quarter == 3)
    def _():
        signal(ready.at[1], beside(last), ba)

    def far_copy(side, chunk):
        return pltpu.make_async_remote_copy(
            src_ref=u_hbm.at[piece(chunk)], dst_ref=far.at[1 - side, piece(chunk)],
            send_sem=far_send.at[side, chunk], recv_sem=far_recv.at[1 - side, chunk],
            device_id=(beside(side), ba), device_id_type=MESH)

    def far_arrived(side, chunk):
        pltpu.make_async_remote_copy(
            src_ref=u_hbm.at[piece(chunk)], dst_ref=far.at[side, piece(chunk)],
            send_sem=far_send.at[side, chunk], recv_sem=far_recv.at[side, chunk],
            device_id=(beside(side), ba), device_id_type=MESH).wait_recv()

    def near_copy(side, match, chunk):
        return pltpu.make_async_remote_copy(
            src_ref=far.at[side, piece(chunk)], dst_ref=near.at[side, match, piece(chunk)],
            send_sem=near_send.at[side, match, chunk], recv_sem=near_recv.at[side, match, chunk],
            device_id=(ka, partners[match]), device_id_type=MESH)

    def send(side):
        for chunk in range(CHUNKS):
            far_copy(side, chunk).start()

    def forward(side, chunk):
        far_arrived(side, chunk)
        for match in reversed(range(MATCHES)):
            near_copy(side, match, chunk).start()

    @pl.when(quarter == 0)
    def _():
        pl.semaphore_wait(ready.at[0], 1)

    send(first)

    @pl.when(quarter == 3)
    def _():
        send(last)

    loads[1].wait()

    def coord(k, axis):
        return coords[axis, k].astype(F32)

    below, above = beside(0), beside(1)
    kern[0] = coulomb([(coord(ka, a) - coord(below, a)) * 0.25 for a in range(3)], False)
    kern[1] = coulomb([(coord(above, a) - coord(ka, a)) * 0.25 for a in range(3)], True)
    loads[0].wait()
    for c in range(BLOCKS):
        raw[0, pairs(c), :] = u_raw[pairs(c), :].astype(F32)
    for c in range(BLOCKS):
        own[0, part(c), :] = raw[0, reals(c), :]
        own[1, part(c), :] = raw[0, imags(c), :]
    for load in loads[2:]:
        load.wait()

    def take(lead, hold):
        taken = 0
        for chunk in range(CHUNKS):
            if chunk == hold:
                pl.semaphore_wait(ready.at[1], 1)
                send(last)
            if chunk >= lead:
                forward(last, taken)
                taken += 1
            forward(first, chunk)
        for chunk in range(taken, CHUNKS):
            forward(last, chunk)

    for number, lead in enumerate(LEADS):
        @pl.when(quarter == number)
        def _():
            take(lead, HOLDS[number] if number < 3 else None)

    def lanes(match):
        return pl.ds(match * LANES, LANES)

    def rows(match, c):
        return pl.ds(match * ROWS + c * PART, PART)

    def densities(side):
        for match in range(MATCHES):
            for chunk in range(CHUNKS):
                near_copy(side, match, chunk).wait_recv()
            for c in range(BLOCKS):
                raw[match, pairs(c), :] = near[side, match, pairs(c), :].astype(F32)
            for c in range(BLOCKS):
                ur, ui = own[0, part(c), :], own[1, part(c), :]
                vr, vi = raw[match, reals(c), :], raw[match, imags(c), :]
                xs[part(c), lanes(match)] = (ur * vr + ui * vi).astype(BF16)
                xs[part(BLOCKS + c), lanes(match)] = (ui * vr - ur * vi).astype(BF16)

    def turn_in():
        for match in range(MATCHES):
            for c in range(BLOCKS):
                zr, zi = zs[part(c), lanes(match)], zs[part(BLOCKS + c), lanes(match)]
                ys[rows(match, c), :LANES] = (zr * tab_turn[0] + zi * tab_turn[1]).astype(BF16)
                ys[rows(match, c), LANES:] = (zi * tab_turn[0] - zr * tab_turn[1]).astype(BF16)

    def screen(side):
        for match in range(MATCHES):
            for c in range(BLOCKS):
                scale = kern[side, part(c), :]
                ys[rows(match, c), :LANES] = (fs[rows(match, c), :LANES] * scale).astype(BF16)
                ys[rows(match, c), LANES:] = (fs[rows(match, c), LANES:] * scale).astype(BF16)

    def turn_back():
        for match in range(MATCHES):
            for c in range(BLOCKS):
                fr, fi = fs[rows(match, c), :LANES], fs[rows(match, c), LANES:]
                xs[part(c), lanes(match)] = (fr * tab_turn[0] - fi * tab_turn[1]).astype(BF16)
                xs[part(BLOCKS + c), lanes(match)] = (fi * tab_turn[0] + fr * tab_turn[1]).astype(BF16)

    def product(target, left, right):
        target[...] = jnp.dot(left[...], right[...], preferred_element_type=F32)

    def apply(final):
        for c in range(BLOCKS):
            real = total[0, part(c), :] if final else jnp.zeros((PART, LANES), F32)
            imag = total[1, part(c), :] if final else jnp.zeros((PART, LANES), F32)
            for match in range(MATCHES):
                vr, vi = raw[match, reals(c), :], raw[match, imags(c), :]
                wr, wi = zs[part(c), lanes(match)], zs[part(BLOCKS + c), lanes(match)]
                real = real + (vi * wi - vr * wr)
                imag = imag - (vr * wi + vi * wr)
            if final:
                out_ref[reals(c), :] = real
                out_ref[imags(c), :] = imag
            else:
                total[0, part(c), :] = real
                total[1, part(c), :] = imag

    def stages(side, final):
        return (
            lambda: densities(side),
            lambda: product(zs, tab_rf, xs),
            turn_in,
            lambda: product(fs, ys, tab_lf),
            lambda: screen(side),
            lambda: product(fs, ys, tab_li),
            lambda: (turn_back(), product(zs, tab_ri, xs)),
            lambda: apply(final),
        )

    for stage in stages(first, False):
        stage()
    for stage in stages(last, True):
        stage()

    for side in range(2):
        for chunk in range(CHUNKS):
            far_copy(side, chunk).wait_send()
            for match in range(MATCHES):
                near_copy(side, match, chunk).wait_send()


def per_device(orbitals, kpoint_coords):
    kpoints = lax.axis_size("ka")
    own = orbitals.reshape(2, ROWS, LANES).transpose(1, 0, 2).reshape(2 * ROWS, LANES)
    whole = pl.BlockSpec(memory_space=pltpu.HBM)
    sems = pltpu.SemaphoreType.DMA
    tables = waves()
    out = pl.pallas_call(
        functools.partial(kernel, kpoints),
        out_shape=jax.ShapeDtypeStruct((2 * ROWS, LANES), F32),
        in_specs=[whole] * (2 + len(tables)),
        out_specs=pl.BlockSpec(memory_space=pltpu.VMEM),
        scratch_shapes=[
            pltpu.VMEM((2 * ROWS, 2 * ROWS), BF16),
            pltpu.VMEM((2 * LANES, 2 * LANES), BF16),
            pltpu.VMEM((2 * LANES, 2 * LANES), BF16),
            pltpu.VMEM((2 * ROWS, 2 * ROWS), BF16),
            pltpu.VMEM((2, PART, LANES), F32),
            pltpu.SMEM((3, kpoints), jnp.int32),
            pltpu.VMEM((2 * ROWS, LANES), BF16),
            pltpu.VMEM((2, 2 * ROWS, LANES), BF16),
            pltpu.VMEM((2, MATCHES, 2 * ROWS, LANES), BF16),
            pltpu.VMEM((2, ROWS, LANES), F32),
            pltpu.VMEM((MATCHES, 2 * ROWS, LANES), F32),
            pltpu.VMEM((2, ROWS, LANES), F32),
            pltpu.VMEM((2, ROWS, LANES), F32),
            pltpu.VMEM((2 * ROWS, MATCHES * LANES), BF16),
            pltpu.VMEM((2 * ROWS, MATCHES * LANES), F32),
            pltpu.VMEM((MATCHES * ROWS, 2 * LANES), BF16),
            pltpu.VMEM((MATCHES * ROWS, 2 * LANES), F32),
            sems((7,)),
            sems((2, CHUNKS)),
            sems((2, CHUNKS)),
            sems((2, MATCHES, CHUNKS)),
            sems((2, MATCHES, CHUNKS)),
            pltpu.SemaphoreType.REGULAR((2,)),
        ],
        compiler_params=pltpu.CompilerParams(collective_id=COLLECTIVE, has_side_effects=True, vmem_limit_bytes=VMEM),
    )(*(pltpu.with_memory_space_constraint(a, pltpu.HBM) for a in (own, kpoint_coords.T, *tables)))
    return out.reshape(ROWS, 2, LANES).transpose(1, 0, 2).reshape(1, 1, 2, GRID**3)


def solution(mesh):
    return jax.shard_map(
        per_device,
        mesh=mesh,
        in_specs=(P("ka", "ba", None, None), P()),
        out_specs=P("ka", "ba", None, None),
        check_vma=False,
    )
```
